32 devices in a mesh: grp: 1, rows: 32 (over z, y, x, core).
Axes of the slice: x: 2, y: 2, z: 4, core: 2. Of those that a mesh axis runs over, the one named last changes fastest.
Arguments:
- embeddings: bfloat16 [16384, 1024], P(('grp', 'rows')), may hold values from -30 to 30
- centroids: bfloat16 [4096, 1024], replicated, may hold values from -0.1875 to 0.1875
- log_weights: float32 [4096], replicated, may hold values from -1 to 1
Outputs:
- new_centroids: bfloat16 [4096, 1024], P(('grp', 'rows'))
- new_log_weights: float32 [4096], P(('grp', 'rows'))
- log_normalizer: float32 [16384], P(('grp', 'rows'))
The draws below stay inside these ranges and needn't reach their ends.
All inputs are finite; a program needn't handle non-finite values.
Results may differ from the reference program's by a relative error of at most 0.0034.
Values may be sent and summed in bfloat16 or wider, within the bound.
A program may use at most 128 MiB of HBM per device.

```python
import math
import jax
import jax.numpy as jnp
from jax import lax

D = 1024
K = 4096
KAPPA = 32
ROWS_DEV = 512
NROWS = 16384


def draw_embeddings(key, part):
    key_noise = jax.random.fold_in(key, 11)
    key_topic = jax.random.fold_in(key, 12)
    key_rowscale = jax.random.fold_in(key, 13)
    key_colscale = jax.random.fold_in(key, 14)
    blocks_count = NROWS // ROWS_DEV
    noise_draw = jax.random.normal(key_noise, (blocks_count, ROWS_DEV, D), jnp.float32)
    topic_draw = jax.random.normal(key_topic, (blocks_count, 1, D), jnp.float32)
    row_scale = jnp.exp(jax.random.uniform(key_rowscale, (blocks_count, ROWS_DEV, 1), jnp.float32, math.log(0.3), math.log(3.0)))
    col_scale = jnp.exp(jax.random.uniform(key_colscale, (1, 1, D), jnp.float32, math.log(0.5), math.log(2.0)))
    base_draw = 0.6 * noise_draw + 0.8 * topic_draw
    values = jnp.clip(base_draw * row_scale * col_scale, -30.0, 30.0)
    return values.reshape(NROWS, D).astype(jnp.bfloat16)


def centred(own_key, dims, spread, limit, kind=jnp.bfloat16):
    return jnp.clip(spread * jax.random.normal(own_key, dims, jnp.float32), -limit, limit).astype(kind)


def setup_inputs(seed: int = 0, part: int = 0) -> dict:
    seeds = jax.random.split(jax.random.key(seed), 4)
    part_keys = jax.random.split(jax.random.fold_in(seeds[3], part), 4)
    return {
        "embeddings": draw_embeddings(jax.random.fold_in(jax.random.fold_in(seeds[3], part), 71), part),
        "centroids": centred(seeds[1], (K, D), D ** -0.5, 0.1875),
        "log_weights": jnp.clip(jax.random.uniform(seeds[2], (K,), jnp.float32, -1.0, 1.0), -1.0, 1.0),
    }


def reference(embeddings, centroids, log_weights):
    embed_float = embeddings.astype(jnp.float32)
    unit_rows = (embed_float * lax.rsqrt(lax.optimization_barrier(jnp.sum(embed_float * embed_float, 1, keepdims=True)) + 1e-06)).astype(jnp.bfloat16)
    blocks = unit_rows.reshape(NROWS // ROWS_DEV, ROWS_DEV, D)

    def accumulate(running_pair, row_block):
        centroid_sum, count_sum = running_pair
        scores = KAPPA * jnp.dot(row_block, centroids.T, preferred_element_type=jnp.float32) + log_weights
        exponent = jnp.exp(scores)
        responsible = (exponent / lax.optimization_barrier(jnp.sum(exponent, 1, keepdims=True))).astype(jnp.bfloat16)
        centroid_sum = centroid_sum + jnp.dot(responsible.T, row_block, preferred_element_type=jnp.float32)
        count_sum = count_sum + lax.optimization_barrier(jnp.sum(responsible.astype(jnp.float32), 0))
        return ((centroid_sum, count_sum), None)
    start_pair = (jnp.zeros((K, D), jnp.float32), jnp.zeros((K,), jnp.float32))
    (centroid_sum, count_sum), unused = lax.scan(accumulate, start_pair, blocks)
    new_directions = (centroid_sum * lax.rsqrt(lax.optimization_barrier(jnp.sum(centroid_sum * centroid_sum, 1, keepdims=True)) + 1e-06)).astype(jnp.bfloat16)
    new_log_weights = jnp.log(count_sum / NROWS)

    def second_pass(row_block):
        scores = KAPPA * jnp.dot(row_block, new_directions.T, preferred_element_type=jnp.float32) + new_log_weights
        return jnp.log(lax.optimization_barrier(jnp.sum(jnp.exp(scores), 1)))
    log_normalizer = lax.map(second_pass, blocks).reshape(NROWS)
    return (new_directions, new_log_weights, log_normalizer)
```

```python
import functools

import jax
import jax.numpy as jnp
from jax import lax
from jax.experimental import pallas as pl
from jax.experimental.pallas import tpu as pltpu
from jax.sharding import PartitionSpec as P

KAPPA = 32
GROUP = 8
MESH = pl.DeviceIdType.MESH
NT = (((1,), (1,)), ((), ()))


def kernel(
    zs, nrows, dchunk, emb_ref, cent_hbm, lw_ref, dir_ref, nlw_ref, lse_ref,
    unit, cent, expo, resp, rsum, rsum_all, send_buf, recv_buf, cnt_send, cnt_recv,
    own_sum, gathered, nlw_all, part, part_recv,
    cent_sem, row_ssem, row_rsem, rs_ssem, rs_rsem, sc_ssem, sc_rsem,
    cn_ssem, cn_rsem, ag_ssem, ag_rsem, nl_ssem, nl_rsem, fin_ssem, fin_rsem,
):
    rows, depth = emb_ref.shape
    half = rows // 2
    comp = dir_ref.shape[0]
    chunks = depth // dchunk
    comps = zs * comp
    me = lax.axis_index("rows")
    z = me // GROUP
    p = me % GROUP

    def plane(mask):
        q = p
        for bit in (1, 2, 4):
            if mask & bit:
                q = q + bit - 2 * bit * ((p // bit) % 2)
        return q

    def dev(zz, q):
        return {"rows": zz * GROUP + q}

    def remote(src, dst, ssem, rsem, to):
        return pltpu.make_async_remote_copy(
            src_ref=src, dst_ref=dst, send_sem=ssem, recv_sem=rsem,
            device_id=to, device_id_type=MESH,
        )

    barrier = pltpu.get_barrier_semaphore()
    for mask in range(1, GROUP):
        pl.semaphore_signal(barrier, inc=1, device_id=dev(z, plane(mask)), device_id_type=MESH)
    for o in range(1, zs):
        pl.semaphore_signal(barrier, inc=1, device_id=dev((z + o) % zs, p), device_id_type=MESH)

    cent_copies = [
        pltpu.make_async_copy(
            cent_hbm.at[pl.ds((b * GROUP + p) * comp, comp)],
            cent.at[pl.ds(b * comp, comp)],
            cent_sem.at[b],
        )
        for b in range(zs)
    ]
    for c in cent_copies:
        c.start()

    embed = emb_ref[...].astype(jnp.float32)
    unit[pl.ds(p * rows, rows), :] = (
        embed * lax.rsqrt(jnp.sum(embed * embed, 1, keepdims=True) + 1e-06)
    ).astype(jnp.bfloat16)
    pl.semaphore_wait(barrier, GROUP - 1 + zs - 1)

    def row_copy(dst, blk, h):
        where = unit.at[pl.ds(plane(blk) * rows + h * half, half)]
        m = blk ^ dst
        return remote(
            where, where, row_ssem.at[m, h], row_rsem.at[m, h], dev(z, plane(dst))
        )

    def arrived(m, h):
        where = unit.at[pl.ds(plane(m) * rows + h * half, half)]
        remote(where, where, row_ssem.at[m, h], row_rsem.at[m, h], dev(z, plane(1))).wait_recv()

    sends = []

    def send(dst, blk, h):
        c = row_copy(dst, blk, h)
        c.start()
        sends.append(c)

    send(2, 0, 0)
    send(4, 0, 1)
    send(1, 0, 0)
    send(2, 0, 1)
    send(4, 0, 0)
    send(1, 0, 1)
    for c in cent_copies:
        c.wait()

    def score(m, h):
        base = plane(m) * rows + h * half
        at = pl.ds(pl.multiple_of(base, half), half)
        dots = lax.dot_general(cent[...], unit[at, :], NT, preferred_element_type=jnp.float32)
        e = jnp.exp(KAPPA * dots + lw_ref[...])
        expo[:, at] = e
        rsum[:, at] = jnp.broadcast_to(jnp.sum(e, 0, keepdims=True), (8, half))

    score(0, 0)
    score(0, 1)
    arrived(2, 0)
    send(4, 2, 0)
    send(1, 2, 0)
    arrived(4, 1)
    send(2, 4, 1)
    send(1, 4, 1)
    for h in (0, 1):
        arrived(1, h)
        score(1, h)
    score(2, 0)
    score(4, 1)
    arrived(2, 1)
    send(1, 2, 1)
    arrived(4, 0)
    send(1, 4, 0)
    score(2, 1)
    score(4, 0)
    for m, h in ((3, 0), (5, 1), (3, 1), (5, 0)):
        arrived(m, h)
        score(m, h)
    for h in (0, 1):
        arrived(6, h)
        send(1, 6, h)
    for h in (0, 1):
        score(6, h)
    for h in (0, 1):
        arrived(7, h)
        score(7, h)

    sum_copies = []
    for m in range(1, GROUP):
        c = remote(rsum, rsum_all.at[m], sc_ssem.at[m], sc_rsem.at[m], dev(z, plane(m)))
        c.start()
        sum_copies.append(c)
    for c in sum_copies:
        c.wait_recv()
    total = rsum[...]
    for m in range(1, GROUP):
        total = total + rsum_all[m]
    rsum_all[0] = 1.0 / total

    def normalise(i, carry):
        at = pl.ds(pl.multiple_of(i * half, half), half)
        inv = rsum_all[0, :, at][:1]
        resp[:, at] = (expo[:, at] * inv).astype(jnp.bfloat16)
        return carry

    lax.fori_loop(0, 2 * GROUP, normalise, 0)

    cnt_copies = []
    ones = jnp.ones((8, GROUP * rows), jnp.bfloat16)
    for b in range(zs):
        cnt_send[b, :, :comp] = lax.dot_general(
            ones, resp[pl.ds(b * comp, comp), :], NT, preferred_element_type=jnp.float32
        )
    for o in range(1, zs):
        to = (z + zs - o) % zs
        c = remote(cnt_send.at[to], cnt_recv.at[o], cn_ssem.at[o], cn_rsem.at[o], dev(to, p))
        c.start()
        cnt_copies.append(c)

    rs_copies = []
    for d in range(chunks):
        cols = pl.ds(d * dchunk, dchunk)
        acc = jnp.dot(resp[...], unit[:, cols], preferred_element_type=jnp.float32)
        expo[:, cols] = acc
        send_buf[d] = acc.astype(jnp.bfloat16).reshape(zs, comp, dchunk)
        for o in range(1, zs):
            to = (z + zs - o) % zs
            c = remote(
                send_buf.at[d, to], recv_buf.at[d, o], rs_ssem.at[d, o], rs_rsem.at[d, o],
                dev(to, p),
            )
            c.start()
            rs_copies.append(c)
        own_sum[:, cols] = expo[pl.ds(pl.multiple_of(z * comp, comp), comp), cols]

    for c in cnt_copies:
        c.wait_recv()
    count = cnt_send[z]
    for o in range(1, zs):
        count = count + cnt_recv[o]
    nlw = jnp.log(count[:, :comp] / nrows)
    nlw_all[z, :, :comp] = nlw
    nlw_ref[...] = nlw[:1]

    square = jnp.zeros((comp, 1), jnp.float32)
    for d in range(chunks):
        cols = pl.ds(d * dchunk, dchunk)
        got = own_sum[:, cols]
        for o in range(1, zs):
            rs_copies[d * (zs - 1) + o - 1].wait_recv()
            got = got + recv_buf[d, o].astype(jnp.float32)
        own_sum[:, cols] = got
        square = square + jnp.sum(got * got, 1, keepdims=True)
    direction = (own_sum[...] * lax.rsqrt(square + 1e-06)).astype(jnp.bfloat16)
    gathered[z] = direction
    dir_ref[...] = direction

    ag_copies = []
    for o in range(1, zs):
        to = dev((z + zs - o) % zs, p)
        c = remote(nlw_all.at[z], nlw_all.at[z], nl_ssem.at[o], nl_rsem.at[o], to)
        c.start()
        ag_copies.append(c)
        c = remote(gathered.at[z], gathered.at[z], ag_ssem.at[o], ag_rsem.at[o], to)
        c.start()
        ag_copies.append(c)

    part[...] = jnp.zeros_like(part)
    for o in range(zs):
        b = (z + o) % zs
        if o:
            remote(
                nlw_all.at[b], nlw_all.at[b], nl_ssem.at[o], nl_rsem.at[o], dev(b, p)
            ).wait_recv()
            remote(
                gathered.at[b], gathered.at[b], ag_ssem.at[o], ag_rsem.at[o], dev(b, p)
            ).wait_recv()
        col = jnp.transpose(jnp.broadcast_to(nlw_all[b, :1, :], (128, 128)))[:comp, :1]

        def second(i, carry):
            at = pl.ds(pl.multiple_of(i * rows, rows), rows)
            dots = lax.dot_general(
                gathered[b], unit[at, :], NT, preferred_element_type=jnp.float32
            )
            e = jnp.exp(KAPPA * dots + col)
            part[i] = part[i] + jnp.sum(e.reshape(comp // 8, 8, rows), 0)
            return carry

        lax.fori_loop(0, GROUP, second, 0)

    fin_copies = []
    for m in range(1, GROUP):
        q = plane(m)
        c = remote(part.at[q], part_recv.at[m], fin_ssem.at[m], fin_rsem.at[m], dev(z, q))
        c.start()
        fin_copies.append(c)
    final = part[p]
    for m in range(1, GROUP):
        fin_copies[m - 1].wait_recv()
        final = final + part_recv[m]
    lse_ref[...] = jnp.log(jnp.sum(final, 0, keepdims=True))

    for c in sends + sum_copies + cnt_copies + rs_copies + ag_copies + fin_copies:
        c.wait_send()


def local(n, embeddings, centroids, log_weights):
    rows, depth = embeddings.shape
    total = centroids.shape[0]
    zs = n // GROUP
    comp = total // n
    comps = zs * comp
    dchunk = 256
    chunks = depth // dchunk
    grows = GROUP * rows
    p = lax.axis_index("rows") % GROUP
    own_lw = lax.dynamic_index_in_dim(
        log_weights.reshape(zs, GROUP, comp), p, 1, keepdims=False
    ).reshape(comps, 1)
    dma = pltpu.SemaphoreType.DMA
    vmem = pl.BlockSpec(memory_space=pltpu.VMEM)
    bf16, f32 = jnp.bfloat16, jnp.float32
    direction, nlw, lse = pl.pallas_call(
        functools.partial(kernel, zs, n * rows, dchunk),
        out_shape=(
            jax.ShapeDtypeStruct((comp, depth), bf16),
            jax.ShapeDtypeStruct((1, comp), f32),
            jax.ShapeDtypeStruct((1, rows), f32),
        ),
        in_specs=[vmem, pl.BlockSpec(memory_space=pl.ANY), vmem],
        out_specs=(vmem, vmem, vmem),
        scratch_shapes=[
            pltpu.VMEM((grows, depth), bf16),
            pltpu.VMEM((comps, depth), bf16),
            pltpu.VMEM((comps, grows), f32),
            pltpu.VMEM((comps, grows), bf16),
            pltpu.VMEM((8, grows), f32),
            pltpu.VMEM((GROUP, 8, grows), f32),
            pltpu.VMEM((chunks, zs, comp, dchunk), bf16),
            pltpu.VMEM((chunks, zs, comp, dchunk), bf16),
            pltpu.VMEM((zs, 8, 128), f32),
            pltpu.VMEM((zs, 8, 128), f32),
            pltpu.VMEM((comp, depth), f32),
            pltpu.VMEM((zs, comp, depth), bf16),
            pltpu.VMEM((zs, 8, 128), f32),
            pltpu.VMEM((GROUP, 8, rows), f32),
            pltpu.VMEM((GROUP, 8, rows), f32),
            dma((zs,)),
            dma((GROUP, 2)), dma((GROUP, 2)),
            dma((chunks, zs)), dma((chunks, zs)),
            dma((GROUP,)), dma((GROUP,)),
            dma((zs,)), dma((zs,)),
            dma((zs,)), dma((zs,)),
            dma((zs,)), dma((zs,)),
            dma((GROUP,)), dma((GROUP,)),
        ],
        compiler_params=pltpu.CompilerParams(
            collective_id=0, has_side_effects=True, vmem_limit_bytes=60 * 1024 * 1024
        ),
    )(embeddings, centroids, own_lw)
    return direction, nlw.reshape(comp), lse.reshape(rows)


def solution(mesh):
    return jax.shard_map(
        functools.partial(local, mesh.shape["rows"]),
        mesh=mesh,
        in_specs=(P(("grp", "rows"), None), P(), P()),
        out_specs=(P(("grp", "rows"), None), P(("grp", "rows")), P(("grp", "rows"))),
        check_vma=False,
    )
```

```python
import functools

import jax
import jax.numpy as jnp
from jax import lax
from jax.experimental import pallas as pl
from jax.experimental.pallas import tpu as pltpu
from jax.sharding import PartitionSpec as P

KAPPA = 32
GROUP = 8
MESH = pl.DeviceIdType.MESH
NT = (((1,), (1,)), ((), ()))


def kernel(
    reps, nrows, dchunk, emb_ref, cent_hbm, lw_ref, dir_ref, nlw_ref, lse_ref,
    unit, cent, expo, resp, rsum, rsum_all, y_send, y_recv, z_send, z_recv, cnt_send, cnt_recv,
    own_sum, gathered, nlw_all, part, part_recv,
    cent_sem, row_ssem, row_rsem, y_ssem, y_rsem, z_ssem, z_rsem, sc_ssem, sc_rsem,
    cn_ssem, cn_rsem, ag_ssem, ag_rsem, own_ssem, own_rsem, fwd_ssem, fwd_rsem,
    nl_ssem, nl_rsem, fin_ssem, fin_rsem,
):
    rows, depth = emb_ref.shape
    half = rows // 2
    comp = dir_ref.shape[0]
    chunks = depth // dchunk
    zs = 2 * reps
    me = lax.axis_index("rows")
    p = me % 4 + 4 * ((me // 8) % 2)
    y = (me // 4) % 2
    h = me // 16
    mine = y * reps + h

    def plane(mask):
        q = p
        for bit in (1, 2, 4):
            if mask & bit:
                q = q + bit - 2 * bit * ((p // bit) % 2)
        return q

    def rank(q, yy, hh):
        return q % 4 + 4 * yy + 8 * (q // 4) + 16 * hh

    def dev(q, yy, hh):
        return {"rows": rank(q, yy, hh)}

    def mate(mask):
        return dev(plane(mask), y, h)

    def replica(o):
        b = (mine + o) % zs
        return dev(p, b // reps, b % reps)

    def remote(src, dst, ssem, rsem, to):
        return pltpu.make_async_remote_copy(
            src_ref=src, dst_ref=dst, send_sem=ssem, recv_sem=rsem,
            device_id=to, device_id_type=MESH,
        )

    barrier = pltpu.get_barrier_semaphore()
    for mask in range(1, GROUP):
        pl.semaphore_signal(barrier, inc=1, device_id=mate(mask), device_id_type=MESH)
    for o in range(1, zs):
        pl.semaphore_signal(barrier, inc=1, device_id=replica(o), device_id_type=MESH)

    cent_copies = [
        pltpu.make_async_copy(
            cent_hbm.at[pl.ds(rank(p, b // reps, b % reps) * comp, comp)],
            cent.at[pl.ds(b * comp, comp)],
            cent_sem.at[b],
        )
        for b in range(zs)
    ]
    for c in cent_copies:
        c.start()

    embed = emb_ref[...].astype(jnp.float32)
    unit[pl.ds(p * rows, rows), :] = (
        embed * lax.rsqrt(jnp.sum(embed * embed, 1, keepdims=True) + 1e-06)
    ).astype(jnp.bfloat16)
    pl.semaphore_wait(barrier, GROUP - 1 + zs - 1)

    def row_copy(dst, blk, hf):
        where = unit.at[pl.ds(plane(blk) * rows + hf * half, half)]
        m = blk ^ dst
        return remote(
            where, where, row_ssem.at[m, hf], row_rsem.at[m, hf], mate(dst)
        )

    def arrived(m, hf):
        where = unit.at[pl.ds(plane(m) * rows + hf * half, half)]
        remote(where, where, row_ssem.at[m, hf], row_rsem.at[m, hf], mate(1)).wait_recv()

    sends = []

    def send(dst, blk, hf):
        c = row_copy(dst, blk, hf)
        c.start()
        sends.append(c)

    send(2, 0, 0)
    send(4, 0, 1)
    send(1, 0, 0)
    send(2, 0, 1)
    send(4, 0, 0)
    send(1, 0, 1)
    for c in cent_copies:
        c.wait()

    def score(m, hf):
        base = plane(m) * rows + hf * half
        at = pl.ds(pl.multiple_of(base, half), half)
        dots = lax.dot_general(cent[...], unit[at, :], NT, preferred_element_type=jnp.float32)
        e = jnp.exp(KAPPA * dots + lw_ref[...])
        expo[:, at] = e
        rsum[pl.ds(plane(m) * 2 + hf, 1), :] = jnp.sum(e, 0, keepdims=True)

    score(0, 0)
    score(0, 1)
    arrived(2, 0)
    send(4, 2, 0)
    send(1, 2, 0)
    arrived(4, 1)
    send(2, 4, 1)
    send(1, 4, 1)
    for hf in (0, 1):
        arrived(1, hf)
        score(1, hf)
    score(2, 0)
    score(4, 1)
    arrived(2, 1)
    send(1, 2, 1)
    arrived(4, 0)
    send(1, 4, 0)
    score(2, 1)
    score(4, 0)
    for m, hf in ((3, 0), (5, 1), (3, 1), (5, 0)):
        arrived(m, hf)
        score(m, hf)
    for hf in (0, 1):
        arrived(6, hf)
        send(1, 6, hf)
    for hf in (0, 1):
        score(6, hf)
    for hf in (0, 1):
        arrived(7, hf)
        score(7, hf)

    sum_copies = []
    for m in range(1, GROUP):
        c = remote(rsum, rsum_all.at[m], sc_ssem.at[m], sc_rsem.at[m], mate(m))
        c.start()
        sum_copies.append(c)
    for c in sum_copies:
        c.wait_recv()
    total = rsum[...]
    for m in range(1, GROUP):
        total = total + rsum_all[m]
    rsum_all[0] = 1.0 / total

    def normalise(i, carry):
        at = pl.ds(pl.multiple_of(i * half, half), half)
        inv = rsum_all[0, pl.ds(i, 1), :]
        resp[:, at] = (expo[:, at] * inv).astype(jnp.bfloat16)
        return carry

    lax.fori_loop(0, 2 * GROUP, normalise, 0)

    cnt_copies = []
    ones = jnp.ones((8, GROUP * rows), jnp.bfloat16)
    for b in range(zs):
        cnt_send[b, :, :comp] = lax.dot_general(
            ones, resp[pl.ds(b * comp, comp), :], NT, preferred_element_type=jnp.float32
        )
    for o in range(1, zs):
        to = (mine + o) % zs
        c = remote(cnt_send.at[to], cnt_recv.at[o], cn_ssem.at[o], cn_rsem.at[o], replica(o))
        c.start()
        cnt_copies.append(c)

    side = reps * comp
    y_copies = []
    for d in range(chunks):
        cols = pl.ds(d * dchunk, dchunk)
        expo[:, cols] = jnp.dot(resp[...], unit[:, cols], preferred_element_type=jnp.float32)
        other = pl.ds(pl.multiple_of((1 - y) * side, side), side)
        y_send[d] = expo[other, cols].astype(jnp.bfloat16)
        c = remote(
            y_send.at[d], y_recv.at[d], y_ssem.at[d], y_rsem.at[d], dev(p, 1 - y, h)
        )
        c.start()
        y_copies.append(c)

    for c in cnt_copies:
        c.wait_recv()
    count = cnt_send[mine]
    for o in range(1, zs):
        count = count + cnt_recv[o]
    nlw = jnp.log(count[:, :comp] / nrows)
    nlw_all[mine, :, :comp] = nlw
    nlw_ref[...] = nlw[:1]
    nl_copies = []
    for o in range(1, zs):
        c = remote(
            nlw_all.at[mine], nlw_all.at[mine], nl_ssem.at[o], nl_rsem.at[o], replica(o)
        )
        c.start()
        nl_copies.append(c)

    def both(d, hh):
        cols = pl.ds(d * dchunk, dchunk)
        kept = expo[pl.ds(pl.multiple_of(y * side + hh * comp, comp), comp), cols]
        return kept + y_recv[d, pl.ds(pl.multiple_of(hh * comp, comp), comp), :].astype(jnp.float32)

    z_copies = []
    for d in range(chunks):
        y_copies[d].wait_recv()
        for o in range(1, reps):
            hh = (h + o) % reps
            z_send[d, o] = both(d, hh).astype(jnp.bfloat16)
            c = remote(
                z_send.at[d, o], z_recv.at[d, o], z_ssem.at[d, o], z_rsem.at[d, o], dev(p, y, hh)
            )
            c.start()
            z_copies.append(c)
        own_sum[:, pl.ds(d * dchunk, dchunk)] = both(d, h)

    square = jnp.zeros((comp, 1), jnp.float32)
    for d in range(chunks):
        cols = pl.ds(d * dchunk, dchunk)
        got = own_sum[:, cols]
        for o in range(1, reps):
            z_copies[d * (reps - 1) + o - 1].wait_recv()
            got = got + z_recv[d, o].astype(jnp.float32)
        own_sum[:, cols] = got
        square = square + jnp.sum(got * got, 1, keepdims=True)
    direction = (own_sum[...] * lax.rsqrt(square + 1e-06)).astype(jnp.bfloat16)
    gathered[mine] = direction
    dir_ref[...] = direction

    hc = comp // 2

    def piece(b, hf):
        return gathered.at[b, pl.ds(hf * hc, hc)]

    ag_copies = []
    for hf in range(2):
        for o in range(1, reps):
            where = piece(mine, hf)
            c = remote(
                where, where, ag_ssem.at[o, hf], ag_rsem.at[o, hf], dev(p, y, (h + o) % reps)
            )
            c.start()
            ag_copies.append(c)
    own_copy = remote(
        gathered.at[mine], gathered.at[mine], own_ssem.at[0], own_rsem.at[0], dev(p, 1 - y, h)
    )
    own_copy.start()

    part[...] = jnp.zeros_like(part)

    def second(b):
        col = jnp.transpose(jnp.broadcast_to(nlw_all[b, :1, :], (128, 128)))[:comp, :1]

        def body(i, carry):
            at = pl.ds(pl.multiple_of(i * rows, rows), rows)
            dots = lax.dot_general(
                gathered[b], unit[at, :], NT, preferred_element_type=jnp.float32
            )
            e = jnp.exp(KAPPA * dots + col)
            part[i] = part[i] + jnp.sum(e.reshape(comp // 8, 8, rows), 0)
            return carry

        lax.fori_loop(0, GROUP, body, 0)

    fwd_copies = []

    def forward(hf):
        for o in range(1, reps):
            where = piece(y * reps + (h + reps - o) % reps, hf)
            remote(where, where, ag_ssem.at[o, hf], ag_rsem.at[o, hf], dev(p, y, (h + o) % reps)).wait_recv()
            c = remote(
                where, where, fwd_ssem.at[o, hf], fwd_rsem.at[o, hf], dev(p, 1 - y, h)
            )
            c.start()
            fwd_copies.append(c)

    second(mine)
    for c in nl_copies:
        c.wait_recv()
    forward(0)
    own_copy.wait_recv()
    second((1 - y) * reps + h)
    forward(1)
    for o in range(1, reps):
        second(y * reps + (h + reps - o) % reps)
    for o in range(1, reps):
        b = (1 - y) * reps + (h + reps - o) % reps
        for hf in range(2):
            where = piece(b, hf)
            remote(where, where, fwd_ssem.at[o, hf], fwd_rsem.at[o, hf], dev(p, 1 - y, h)).wait_recv()
        second(b)

    fin_copies = []
    for m in range(1, GROUP):
        q = plane(m)
        c = remote(part.at[q], part_recv.at[m], fin_ssem.at[m], fin_rsem.at[m], mate(m))
        c.start()
        fin_copies.append(c)
    final = part[p]
    for m in range(1, GROUP):
        fin_copies[m - 1].wait_recv()
        final = final + part_recv[m]
    lse_ref[...] = jnp.log(jnp.sum(final, 0, keepdims=True))

    for c in sends + sum_copies + cnt_copies + y_copies + nl_copies + z_copies:
        c.wait_send()
    for c in ag_copies + [own_copy] + fwd_copies + fin_copies:
        c.wait_send()


def local(n, embeddings, centroids, log_weights):
    rows, depth = embeddings.shape
    total = centroids.shape[0]
    zs = n // GROUP
    comp = total // n
    comps = zs * comp
    dchunk = 256
    chunks = depth // dchunk
    grows = GROUP * rows
    reps = zs // 2
    me = lax.axis_index("rows")
    split = log_weights.reshape(reps, 2, 2, 4, comp)
    split = lax.dynamic_slice(
        split, (0, (me // 8) % 2, 0, me % 4, 0), (reps, 1, 2, 1, comp)
    )
    own_lw = split.reshape(reps, 2, comp).swapaxes(0, 1).reshape(comps, 1)
    dma = pltpu.SemaphoreType.DMA
    vmem = pl.BlockSpec(memory_space=pltpu.VMEM)
    bf16, f32 = jnp.bfloat16, jnp.float32
    direction, nlw, lse = pl.pallas_call(
        functools.partial(kernel, reps, n * rows, dchunk),
        out_shape=(
            jax.ShapeDtypeStruct((comp, depth), bf16),
            jax.ShapeDtypeStruct((1, comp), f32),
            jax.ShapeDtypeStruct((1, rows), f32),
        ),
        in_specs=[vmem, pl.BlockSpec(memory_space=pl.ANY), vmem],
        out_specs=(vmem, vmem, vmem),
        scratch_shapes=[
            pltpu.VMEM((grows, depth), bf16),
            pltpu.VMEM((comps, depth), bf16),
            pltpu.VMEM((comps, grows), f32),
            pltpu.VMEM((comps, grows), bf16),
            pltpu.VMEM((2 * GROUP, rows // 2), f32),
            pltpu.VMEM((GROUP, 2 * GROUP, rows // 2), f32),
            pltpu.VMEM((chunks, reps * comp, dchunk), bf16),
            pltpu.VMEM((chunks, reps * comp, dchunk), bf16),
            pltpu.VMEM((chunks, reps, comp, dchunk), bf16),
            pltpu.VMEM((chunks, reps, comp, dchunk), bf16),
            pltpu.VMEM((zs, 8, 128), f32),
            pltpu.VMEM((zs, 8, 128), f32),
            pltpu.VMEM((comp, depth), f32),
            pltpu.VMEM((zs, comp, depth), bf16),
            pltpu.VMEM((zs, 8, 128), f32),
            pltpu.VMEM((GROUP, 8, rows), f32),
            pltpu.VMEM((GROUP, 8, rows), f32),
            dma((zs,)),
            dma((GROUP, 2)), dma((GROUP, 2)),
            dma((chunks,)), dma((chunks,)),
            dma((chunks, reps)), dma((chunks, reps)),
            dma((GROUP,)), dma((GROUP,)),
            dma((zs,)), dma((zs,)),
            dma((reps, 2)), dma((reps, 2)),
            dma((1,)), dma((1,)),
            dma((reps, 2)), dma((reps, 2)),
            dma((zs,)), dma((zs,)),
            dma((GROUP,)), dma((GROUP,)),
        ],
        compiler_params=pltpu.CompilerParams(
            collective_id=0, has_side_effects=True, vmem_limit_bytes=60 * 1024 * 1024
        ),
    )(embeddings, centroids, own_lw)
    return direction, nlw.reshape(comp), lse.reshape(rows)


def solution(mesh):
    return jax.shard_map(
        functools.partial(local, mesh.shape["rows"]),
        mesh=mesh,
        in_specs=(P(("grp", "rows"), None), P(), P()),
        out_specs=(P(("grp", "rows"), None), P(("grp", "rows")), P(("grp", "rows"))),
        check_vma=False,
    )
```

```python
import functools

import jax
import jax.numpy as jnp
from jax import lax
from jax.experimental import pallas as pl
from jax.experimental.pallas import tpu as pltpu
from jax.sharding import PartitionSpec as P

KAPPA = 32
GROUP = 8
MESH = pl.DeviceIdType.MESH
NT = (((1,), (1,)), ((), ()))


def kernel(
    reps, nrows, dchunk, emb_ref, cent_hbm, lw_ref, dir_ref, nlw_ref, lse_ref,
    unit, cent, expo, resp, rsum, rsum_all, y_send, y_recv, z_send, z_recv, cnt_send, cnt_recv,
    own_sum, gathered, nlw_all, part, part_recv, lw_row, lw_col,
    cent_sem, row_ssem, row_rsem, y_ssem, y_rsem, z_ssem, z_rsem, sc_ssem, sc_rsem,
    cn_ssem, cn_rsem, ag_ssem, ag_rsem, own_ssem, own_rsem, fwd_ssem, fwd_rsem,
    nl_ssem, nl_rsem, fin_ssem, fin_rsem,
):
    rows, depth = emb_ref.shape
    half = rows // 2
    comp = dir_ref.shape[0]
    chunks = depth // dchunk
    zs = 2 * reps
    hc = comp // 2
    me = lax.axis_index("rows")
    p = me % 4 + 4 * ((me // 8) % 2)
    y = (me // 4) % 2
    h = me // 16
    mine = y * reps + h

    def plane(mask):
        q = p
        for bit in (1, 2, 4):
            if mask & bit:
                q = q + bit - 2 * bit * ((p // bit) % 2)
        return q

    def rank(q, yy, hh):
        return q % 4 + 4 * yy + 8 * (q // 4) + 16 * hh

    def dev(q, yy, hh):
        return {"rows": rank(q, yy, hh)}

    def mate(mask):
        return dev(plane(mask), y, h)

    def replica(o):
        b = (mine + o) % zs
        return dev(p, b // reps, b % reps)

    def remote(src, dst, ssem, rsem, to):
        return pltpu.make_async_remote_copy(
            src_ref=src, dst_ref=dst, send_sem=ssem, recv_sem=rsem,
            device_id=to, device_id_type=MESH,
        )

    barrier = pltpu.get_barrier_semaphore()
    for mask in range(1, GROUP):
        pl.semaphore_signal(barrier, inc=1, device_id=mate(mask), device_id_type=MESH)
    for o in range(1, zs):
        pl.semaphore_signal(barrier, inc=1, device_id=replica(o), device_id_type=MESH)

    cent_copies = [
        pltpu.make_async_copy(
            cent_hbm.at[pl.ds(rank(p, b // reps, b % reps) * comp + c * hc, hc)],
            cent.at[pl.ds((c * zs + b) * hc, hc)],
            cent_sem.at[c, b],
        )
        for c in range(2)
        for b in range(zs)
    ]
    for c in cent_copies:
        c.start()

    def column(row):
        return jnp.transpose(jnp.broadcast_to(row, (128, 128)))[:comp, :1]

    for b in range(zs):
        lw_row[:1, :comp] = lw_ref[pl.ds(rank(p, b // reps, b % reps), 1), :]
        col = column(lw_row[:1, :])
        for c in range(2):
            lw_col[pl.ds((c * zs + b) * hc, hc), :] = col[c * hc : (c + 1) * hc]

    embed = emb_ref[...].astype(jnp.float32)
    unit[pl.ds(p * rows, rows), :] = (
        embed * lax.rsqrt(jnp.sum(embed * embed, 1, keepdims=True) + 1e-06)
    ).astype(jnp.bfloat16)
    pl.semaphore_wait(barrier, GROUP - 1 + zs - 1)

    def row_copy(dst, blk, hf):
        where = unit.at[pl.ds(plane(blk) * rows + hf * half, half)]
        m = blk ^ dst
        return remote(
            where, where, row_ssem.at[m, hf], row_rsem.at[m, hf], mate(dst)
        )

    def arrived(m, hf):
        where = unit.at[pl.ds(plane(m) * rows + hf * half, half)]
        remote(where, where, row_ssem.at[m, hf], row_rsem.at[m, hf], mate(1)).wait_recv()

    sends = []

    def send(dst, blk, hf):
        c = row_copy(dst, blk, hf)
        c.start()
        sends.append(c)

    send(2, 0, 0)
    send(4, 0, 1)
    send(1, 0, 0)
    send(2, 0, 1)
    send(4, 0, 0)
    send(1, 0, 1)
    for c in cent_copies:
        c.wait()

    def score(m, hf):
        base = plane(m) * rows + hf * half
        at = pl.ds(pl.multiple_of(base, half), half)
        dots = lax.dot_general(cent[...], unit[at, :], NT, preferred_element_type=jnp.float32)
        e = jnp.exp(KAPPA * dots + lw_col[...])
        expo[:, at] = e
        rsum[pl.ds(plane(m) * 2 + hf, 1), :] = jnp.sum(e, 0, keepdims=True)

    score(0, 0)
    score(0, 1)
    arrived(2, 0)
    send(4, 2, 0)
    send(1, 2, 0)
    arrived(4, 1)
    send(2, 4, 1)
    send(1, 4, 1)
    for hf in (0, 1):
        arrived(1, hf)
        score(1, hf)
    score(2, 0)
    score(4, 1)
    arrived(2, 1)
    send(1, 2, 1)
    arrived(4, 0)
    send(1, 4, 0)
    score(2, 1)
    score(4, 0)
    for m, hf in ((3, 0), (5, 1), (3, 1), (5, 0)):
        arrived(m, hf)
        score(m, hf)
    for hf in (0, 1):
        arrived(6, hf)
        send(1, 6, hf)
    for hf in (0, 1):
        score(6, hf)
    for hf in (0, 1):
        arrived(7, hf)
        score(7, hf)

    sum_copies = []
    for m in range(1, GROUP):
        c = remote(rsum, rsum_all.at[m], sc_ssem.at[m], sc_rsem.at[m], mate(m))
        c.start()
        sum_copies.append(c)
    for c in sum_copies:
        c.wait_recv()
    total = rsum[...]
    for m in range(1, GROUP):
        total = total + rsum_all[m]
    rsum_all[0] = 1.0 / total

    def normalise(i, carry):
        at = pl.ds(pl.multiple_of(i * half, half), half)
        inv = rsum_all[0, pl.ds(i, 1), :]
        resp[:, at] = (expo[:, at] * inv).astype(jnp.bfloat16)
        return carry

    lax.fori_loop(0, 2 * GROUP, normalise, 0)

    side = reps * hc
    y_copies = {}
    for c in range(2):
        for d in range(chunks):
            cols = pl.ds(d * dchunk, dchunk)
            expo[pl.ds(c * zs * hc, zs * hc), cols] = jnp.dot(
                resp[pl.ds(c * zs * hc, zs * hc), :], unit[:, cols],
                preferred_element_type=jnp.float32,
            )
            other = pl.ds(pl.multiple_of(c * zs * hc + (1 - y) * side, side), side)
            y_send[c, d] = expo[other, cols].astype(jnp.bfloat16)
            y_copies[c, d] = remote(
                y_send.at[c, d], y_recv.at[c, d], y_ssem.at[c, d], y_rsem.at[c, d],
                dev(p, 1 - y, h),
            )
            y_copies[c, d].start()

    cnt_copies = []
    ones = jnp.ones((8, GROUP * rows), jnp.bfloat16)
    for b in range(zs):
        for c in range(2):
            cnt_send[b, :, c * hc : (c + 1) * hc] = lax.dot_general(
                ones, resp[pl.ds((c * zs + b) * hc, hc), :], NT,
                preferred_element_type=jnp.float32,
            )
    for o in range(1, zs):
        to = (mine + o) % zs
        c = remote(cnt_send.at[to], cnt_recv.at[o], cn_ssem.at[o], cn_rsem.at[o], replica(o))
        c.start()
        cnt_copies.append(c)

    def both(c, d, hh):
        cols = pl.ds(d * dchunk, dchunk)
        kept = expo[pl.ds(pl.multiple_of(c * zs * hc + y * side + hh * hc, hc), hc), cols]
        return kept + y_recv[c, d, pl.ds(pl.multiple_of(hh * hc, hc), hc), :].astype(jnp.float32)

    z_copies = {}

    def over_z(c):
        for d in range(chunks):
            y_copies[c, d].wait_recv()
            for o in range(1, reps):
                hh = (h + o) % reps
                z_send[c, d, o] = both(c, d, hh).astype(jnp.bfloat16)
                z_copies[c, d, o] = remote(
                    z_send.at[c, d, o], z_recv.at[c, d, o], z_ssem.at[c, d, o],
                    z_rsem.at[c, d, o], dev(p, y, hh),
                )
                z_copies[c, d, o].start()
            own_sum[pl.ds(c * hc, hc), pl.ds(d * dchunk, dchunk)] = both(c, d, h)

    def piece(b, c):
        return gathered.at[b, pl.ds(c * hc, hc)]

    ag_copies = []
    own_copies = []

    def finish(c):
        here = pl.ds(c * hc, hc)
        square = jnp.zeros((hc, 1), jnp.float32)
        for d in range(chunks):
            cols = pl.ds(d * dchunk, dchunk)
            got = own_sum[here, cols]
            for o in range(1, reps):
                z_copies[c, d, o].wait_recv()
                got = got + z_recv[c, d, o].astype(jnp.float32)
            own_sum[here, cols] = got
            square = square + jnp.sum(got * got, 1, keepdims=True)
        direction = (own_sum[here, :] * lax.rsqrt(square + 1e-06)).astype(jnp.bfloat16)
        gathered[mine, here, :] = direction
        dir_ref[here, :] = direction
        where = piece(mine, c)
        for o in range(1, reps):
            copy = remote(
                where, where, ag_ssem.at[o, c], ag_rsem.at[o, c], dev(p, y, (h + o) % reps)
            )
            copy.start()
            ag_copies.append(copy)
        copy = remote(where, where, own_ssem.at[c], own_rsem.at[c], dev(p, 1 - y, h))
        copy.start()
        own_copies.append(copy)

    over_z(0)
    for c in cnt_copies:
        c.wait_recv()
    count = cnt_send[mine]
    for o in range(1, zs):
        count = count + cnt_recv[o]
    nlw = jnp.log(count[:, :comp] / nrows)
    nlw_all[mine, :, :comp] = nlw
    nlw_ref[...] = nlw[:1]
    nl_copies = []
    for o in range(1, zs):
        c = remote(
            nlw_all.at[mine], nlw_all.at[mine], nl_ssem.at[o], nl_rsem.at[o], replica(o)
        )
        c.start()
        nl_copies.append(c)
    finish(0)
    over_z(1)
    finish(1)

    part[...] = jnp.zeros_like(part)

    def second(b):
        col = column(nlw_all[b, :1, :])

        def body(i, carry):
            at = pl.ds(pl.multiple_of(i * rows, rows), rows)
            dots = lax.dot_general(
                gathered[b], unit[at, :], NT, preferred_element_type=jnp.float32
            )
            e = jnp.exp(KAPPA * dots + col)
            part[i] = part[i] + jnp.sum(e.reshape(comp // 8, 8, rows), 0)
            return carry

        lax.fori_loop(0, GROUP, body, 0)

    fwd_copies = []

    def forward(hf):
        for o in range(1, reps):
            where = piece(y * reps + (h + reps - o) % reps, hf)
            remote(where, where, ag_ssem.at[o, hf], ag_rsem.at[o, hf], dev(p, y, (h + o) % reps)).wait_recv()
            c = remote(
                where, where, fwd_ssem.at[o, hf], fwd_rsem.at[o, hf], dev(p, 1 - y, h)
            )
            c.start()
            fwd_copies.append(c)

    forward(0)
    second(mine)
    for c in nl_copies + own_copies:
        c.wait_recv()
    second((1 - y) * reps + h)
    forward(1)
    for o in range(1, reps):
        second(y * reps + (h + reps - o) % reps)
    for o in range(1, reps):
        b = (1 - y) * reps + (h + reps - o) % reps
        for hf in range(2):
            where = piece(b, hf)
            remote(where, where, fwd_ssem.at[o, hf], fwd_rsem.at[o, hf], dev(p, 1 - y, h)).wait_recv()
        second(b)

    fin_copies = []
    for m in range(1, GROUP):
        q = plane(m)
        c = remote(part.at[q], part_recv.at[m], fin_ssem.at[m], fin_rsem.at[m], mate(m))
        c.start()
        fin_copies.append(c)
    final = part[p]
    for m in range(1, GROUP):
        fin_copies[m - 1].wait_recv()
        final = final + part_recv[m]
    lse_ref[...] = jnp.sum(final, 0, keepdims=True)

    for c in sends + sum_copies + cnt_copies + nl_copies:
        c.wait_send()
    for c in list(y_copies.values()) + list(z_copies.values()):
        c.wait_send()
    for c in ag_copies + own_copies + fwd_copies + fin_copies:
        c.wait_send()


def settle(direction, nlw, lse, direction_out, nlw_out, lse_out):
    direction_out[...] = direction[...]
    nlw_out[...] = nlw[...]
    lse_out[...] = jnp.log(lse[...])


def local(n, embeddings, centroids, log_weights):
    rows, depth = embeddings.shape
    total = centroids.shape[0]
    zs = n // GROUP
    comp = total // n
    comps = zs * comp
    dchunk = 256
    chunks = depth // dchunk
    grows = GROUP * rows
    reps = zs // 2
    hc = comp // 2
    dma = pltpu.SemaphoreType.DMA
    vmem = pl.BlockSpec(memory_space=pltpu.VMEM)
    bf16, f32 = jnp.bfloat16, jnp.float32
    direction, nlw, lse = pl.pallas_call(
        functools.partial(kernel, reps, n * rows, dchunk),
        out_shape=(
            jax.ShapeDtypeStruct((comp, depth), bf16),
            jax.ShapeDtypeStruct((1, comp), f32),
            jax.ShapeDtypeStruct((1, rows), f32),
        ),
        in_specs=[vmem, pl.BlockSpec(memory_space=pl.ANY), vmem],
        out_specs=(vmem, vmem, vmem),
        scratch_shapes=[
            pltpu.VMEM((grows, depth), bf16),
            pltpu.VMEM((comps, depth), bf16),
            pltpu.VMEM((comps, grows), f32),
            pltpu.VMEM((comps, grows), bf16),
            pltpu.VMEM((2 * GROUP, rows // 2), f32),
            pltpu.VMEM((GROUP, 2 * GROUP, rows // 2), f32),
            pltpu.VMEM((2, chunks, reps * hc, dchunk), bf16),
            pltpu.VMEM((2, chunks, reps * hc, dchunk), bf16),
            pltpu.VMEM((2, chunks, reps, hc, dchunk), bf16),
            pltpu.VMEM((2, chunks, reps, hc, dchunk), bf16),
            pltpu.VMEM((zs, 8, 128), f32),
            pltpu.VMEM((zs, 8, 128), f32),
            pltpu.VMEM((comp, depth), f32),
            pltpu.VMEM((zs, comp, depth), bf16),
            pltpu.VMEM((zs, 8, 128), f32),
            pltpu.VMEM((GROUP, 8, rows), f32),
            pltpu.VMEM((GROUP, 8, rows), f32),
            pltpu.VMEM((8, 128), f32),
            pltpu.VMEM((comps, 1), f32),
            dma((2, zs)),
            dma((GROUP, 2)), dma((GROUP, 2)),
            dma((2, chunks)), dma((2, chunks)),
            dma((2, chunks, reps)), dma((2, chunks, reps)),
            dma((GROUP,)), dma((GROUP,)),
            dma((zs,)), dma((zs,)),
            dma((reps, 2)), dma((reps, 2)),
            dma((2,)), dma((2,)),
            dma((reps, 2)), dma((reps, 2)),
            dma((zs,)), dma((zs,)),
            dma((GROUP,)), dma((GROUP,)),
        ],
        compiler_params=pltpu.CompilerParams(
            collective_id=0, has_side_effects=True, vmem_limit_bytes=60 * 1024 * 1024
        ),
    )(embeddings, centroids, log_weights.reshape(n, comp))
    direction, nlw, lse = pl.pallas_call(
        settle,
        out_shape=(
            jax.ShapeDtypeStruct((comp, depth), bf16),
            jax.ShapeDtypeStruct((1, comp), f32),
            jax.ShapeDtypeStruct((1, rows), f32),
        ),
        in_specs=[vmem, vmem, vmem],
        out_specs=(vmem, vmem, vmem),
    )(direction, nlw, lse)
    return direction, nlw.reshape(comp), lse.reshape(rows)


def solution(mesh):
    return jax.shard_map(
        functools.partial(local, mesh.shape["rows"]),
        mesh=mesh,
        in_specs=(P(("grp", "rows"), None), P(), P()),
        out_specs=(P(("grp", "rows"), None), P(("grp", "rows")), P(("grp", "rows"))),
        check_vma=False,
    )
```

```python
import functools

import jax
import jax.numpy as jnp
from jax import lax
from jax.experimental import pallas as pl
from jax.experimental.pallas import tpu as pltpu
from jax.sharding import PartitionSpec as P

KAPPA = 32
GROUP = 8
MESH = pl.DeviceIdType.MESH
NT = (((1,), (1,)), ((), ()))


def kernel(
    reps, nrows, dchunk, emb_ref, cent_hbm, lw_ref, dir_ref, nlw_ref, lse_ref,
    unit, cent, expo, resp, rsum, rsum_all, y_send, y_recv, z_send, z_recv, cnt_send, cnt_recv,
    own_sum, gathered, nlw_all, part, part_recv, lw_row, lw_col,
    cent_sem, row_ssem, row_rsem, y_ssem, y_rsem, z_ssem, z_rsem, sc_ssem, sc_rsem,
    cn_ssem, cn_rsem, ag_ssem, ag_rsem, own_ssem, own_rsem, fwd_ssem, fwd_rsem,
    nl_ssem, nl_rsem, fin_ssem, fin_rsem,
):
    rows, depth = emb_ref.shape
    half = rows // 2
    comp = dir_ref.shape[0]
    chunks = depth // dchunk
    zs = 2 * reps
    hc = comp // 2
    me = lax.axis_index("rows")
    p = me % 4 + 4 * ((me // 8) % 2)
    y = (me // 4) % 2
    h = me // 16
    mine = y * reps + h

    def plane(mask):
        q = p
        for bit in (1, 2, 4):
            if mask & bit:
                q = q + bit - 2 * bit * ((p // bit) % 2)
        return q

    def rank(q, yy, hh):
        return q % 4 + 4 * yy + 8 * (q // 4) + 16 * hh

    def dev(q, yy, hh):
        return {"rows": rank(q, yy, hh)}

    def mate(mask):
        return dev(plane(mask), y, h)

    def replica(o):
        b = (mine + o) % zs
        return dev(p, b // reps, b % reps)

    def remote(src, dst, ssem, rsem, to):
        return pltpu.make_async_remote_copy(
            src_ref=src, dst_ref=dst, send_sem=ssem, recv_sem=rsem,
            device_id=to, device_id_type=MESH,
        )

    barrier = pltpu.get_barrier_semaphore()
    for mask in range(1, GROUP):
        pl.semaphore_signal(barrier, inc=1, device_id=mate(mask), device_id_type=MESH)
    for o in range(1, zs):
        pl.semaphore_signal(barrier, inc=1, device_id=replica(o), device_id_type=MESH)

    cent_copies = [
        pltpu.make_async_copy(
            cent_hbm.at[pl.ds(rank(p, b // reps, b % reps) * comp + c * hc, hc)],
            cent.at[pl.ds((c * zs + b) * hc, hc)],
            cent_sem.at[c, b],
        )
        for c in range(2)
        for b in range(zs)
    ]
    for c in cent_copies:
        c.start()

    def column(row):
        return jnp.transpose(jnp.broadcast_to(row, (128, 128)))[:comp, :1]

    def unit_half(hf):
        here = pl.ds(hf * half, half)
        embed = emb_ref[here, :].astype(jnp.float32)
        unit[pl.ds(pl.multiple_of(p * rows + hf * half, half), half), :] = (
            embed * lax.rsqrt(jnp.sum(embed * embed, 1, keepdims=True) + 1e-06)
        ).astype(jnp.bfloat16)

    unit_half(0)
    pl.semaphore_wait(barrier, GROUP - 1 + zs - 1)

    def row_copy(dst, blk, hf):
        where = unit.at[pl.ds(plane(blk) * rows + hf * half, half)]
        m = blk ^ dst
        return remote(
            where, where, row_ssem.at[m, hf], row_rsem.at[m, hf], mate(dst)
        )

    def arrived(m, hf):
        where = unit.at[pl.ds(plane(m) * rows + hf * half, half)]
        remote(where, where, row_ssem.at[m, hf], row_rsem.at[m, hf], mate(1)).wait_recv()

    sends = []

    def send(dst, blk, hf):
        c = row_copy(dst, blk, hf)
        c.start()
        sends.append(c)

    for hf in (0, 1):
        if hf:
            unit_half(hf)
        send(2, 0, hf)
        send(4, 0, hf)
        send(1, 0, hf)
    for b in range(zs):
        lw_row[:1, :comp] = lw_ref[pl.ds(rank(p, b // reps, b % reps), 1), :]
        col = column(lw_row[:1, :])
        for c in range(2):
            lw_col[pl.ds((c * zs + b) * hc, hc), :] = col[c * hc : (c + 1) * hc]
    for c in cent_copies:
        c.wait()

    def score(m, hf):
        base = plane(m) * rows + hf * half
        at = pl.ds(pl.multiple_of(base, half), half)
        dots = lax.dot_general(cent[...], unit[at, :], NT, preferred_element_type=jnp.float32)
        e = jnp.exp(KAPPA * dots + lw_col[...])
        expo[:, at] = e
        rsum[pl.ds(plane(m) * 2 + hf, 1), :] = jnp.sum(e, 0, keepdims=True)

    score(0, 0)
    score(0, 1)
    arrived(2, 0)
    send(4, 2, 0)
    send(1, 2, 0)
    arrived(4, 1)
    send(2, 4, 1)
    send(1, 4, 1)
    for hf in (0, 1):
        arrived(1, hf)
        score(1, hf)
    score(2, 0)
    score(4, 1)
    arrived(2, 1)
    send(1, 2, 1)
    arrived(4, 0)
    send(1, 4, 0)
    score(2, 1)
    score(4, 0)
    for m, hf in ((3, 0), (5, 1), (3, 1), (5, 0)):
        arrived(m, hf)
        score(m, hf)
    for hf in (0, 1):
        arrived(6, hf)
        send(1, 6, hf)
    for hf in (0, 1):
        score(6, hf)
    for hf in (0, 1):
        arrived(7, hf)
        score(7, hf)

    sum_copies = []
    for m in range(1, GROUP):
        c = remote(rsum, rsum_all.at[m], sc_ssem.at[m], sc_rsem.at[m], mate(m))
        c.start()
        sum_copies.append(c)
    for c in sum_copies:
        c.wait_recv()
    total = rsum[...]
    for m in range(1, GROUP):
        total = total + rsum_all[m]
    rsum_all[0] = 1.0 / total

    def normalise(i, carry):
        at = pl.ds(pl.multiple_of(i * half, half), half)
        inv = rsum_all[0, pl.ds(i, 1), :]
        resp[:, at] = (expo[:, at] * inv).astype(jnp.bfloat16)
        return carry

    lax.fori_loop(0, 2 * GROUP, normalise, 0)

    side = reps * hc
    y_copies = {}
    def both(c, d, hh):
        cols = pl.ds(d * dchunk, dchunk)
        kept = expo[pl.ds(pl.multiple_of(c * zs * hc + y * side + hh * hc, hc), hc), cols]
        return kept + y_recv[c, d, pl.ds(pl.multiple_of(hh * hc, hc), hc), :].astype(jnp.float32)

    z_copies = {}

    def over_z(c, d):
        y_copies[c, d].wait_recv()
        for o in range(1, reps):
            hh = (h + o) % reps
            z_send[c, d, o] = both(c, d, hh).astype(jnp.bfloat16)
            z_copies[c, d, o] = remote(
                z_send.at[c, d, o], z_recv.at[c, d, o], z_ssem.at[c, d, o],
                z_rsem.at[c, d, o], dev(p, y, hh),
            )
            z_copies[c, d, o].start()
        own_sum[pl.ds(c * hc, hc), pl.ds(d * dchunk, dchunk)] = both(c, d, h)

    for c in range(2):
        for d in range(chunks):
            cols = pl.ds(d * dchunk, dchunk)
            expo[pl.ds(c * zs * hc, zs * hc), cols] = jnp.dot(
                resp[pl.ds(c * zs * hc, zs * hc), :], unit[:, cols],
                preferred_element_type=jnp.float32,
            )
            other = pl.ds(pl.multiple_of(c * zs * hc + (1 - y) * side, side), side)
            y_send[c, d] = expo[other, cols].astype(jnp.bfloat16)
            y_copies[c, d] = remote(
                y_send.at[c, d], y_recv.at[c, d], y_ssem.at[c, d], y_rsem.at[c, d],
                dev(p, 1 - y, h),
            )
            y_copies[c, d].start()
            if c:
                over_z(0, d)

    cnt_copies = []
    ones = jnp.ones((8, GROUP * rows), jnp.bfloat16)
    for b in range(zs):
        for c in range(2):
            cnt_send[b, :, c * hc : (c + 1) * hc] = lax.dot_general(
                ones, resp[pl.ds((c * zs + b) * hc, hc), :], NT,
                preferred_element_type=jnp.float32,
            )
    for o in range(1, zs):
        to = (mine + o) % zs
        c = remote(cnt_send.at[to], cnt_recv.at[o], cn_ssem.at[o], cn_rsem.at[o], replica(o))
        c.start()
        cnt_copies.append(c)

    def piece(b, c):
        return gathered.at[b, pl.ds(c * hc, hc)]

    ag_copies = []
    own_copies = []

    def finish(c):
        here = pl.ds(c * hc, hc)
        square = jnp.zeros((hc, 1), jnp.float32)
        for d in range(chunks):
            cols = pl.ds(d * dchunk, dchunk)
            got = own_sum[here, cols]
            for o in range(1, reps):
                z_copies[c, d, o].wait_recv()
                got = got + z_recv[c, d, o].astype(jnp.float32)
            own_sum[here, cols] = got
            square = square + jnp.sum(got * got, 1, keepdims=True)
        direction = (own_sum[here, :] * lax.rsqrt(square + 1e-06)).astype(jnp.bfloat16)
        gathered[mine, here, :] = direction
        dir_ref[here, :] = direction
        where = piece(mine, c)
        for o in range(1, reps):
            copy = remote(
                where, where, ag_ssem.at[o, c], ag_rsem.at[o, c], dev(p, y, (h + o) % reps)
            )
            copy.start()
            ag_copies.append(copy)
        copy = remote(where, where, own_ssem.at[c], own_rsem.at[c], dev(p, 1 - y, h))
        copy.start()
        own_copies.append(copy)

    finish(0)
    for d in range(chunks):
        over_z(1, d)
    for c in cnt_copies:
        c.wait_recv()
    count = cnt_send[mine]
    for o in range(1, zs):
        count = count + cnt_recv[o]
    nlw = jnp.log(count[:, :comp] / nrows)
    nlw_all[mine, :, :comp] = nlw
    nlw_ref[...] = nlw[:1]
    nl_copies = []
    for o in range(1, zs):
        c = remote(
            nlw_all.at[mine], nlw_all.at[mine], nl_ssem.at[o], nl_rsem.at[o], replica(o)
        )
        c.start()
        nl_copies.append(c)
    finish(1)

    part[...] = jnp.zeros_like(part)

    def second(b):
        col = column(nlw_all[b, :1, :])

        def body(i, carry):
            at = pl.ds(pl.multiple_of(i * rows, rows), rows)
            dots = lax.dot_general(
                gathered[b], unit[at, :], NT, preferred_element_type=jnp.float32
            )
            e = jnp.exp(KAPPA * dots + col)
            part[i] = part[i] + jnp.sum(e.reshape(comp // 8, 8, rows), 0)
            return carry

        lax.fori_loop(0, GROUP, body, 0)

    fwd_copies = []

    def forward(hf):
        for o in range(1, reps):
            where = piece(y * reps + (h + reps - o) % reps, hf)
            remote(where, where, ag_ssem.at[o, hf], ag_rsem.at[o, hf], dev(p, y, (h + o) % reps)).wait_recv()
            c = remote(
                where, where, fwd_ssem.at[o, hf], fwd_rsem.at[o, hf], dev(p, 1 - y, h)
            )
            c.start()
            fwd_copies.append(c)

    forward(0)
    second(mine)
    for c in nl_copies + own_copies:
        c.wait_recv()
    second((1 - y) * reps + h)
    forward(1)
    for o in range(1, reps):
        second(y * reps + (h + reps - o) % reps)
    for o in range(1, reps):
        b = (1 - y) * reps + (h + reps - o) % reps
        for hf in range(2):
            where = piece(b, hf)
            remote(where, where, fwd_ssem.at[o, hf], fwd_rsem.at[o, hf], dev(p, 1 - y, h)).wait_recv()
        second(b)

    fin_copies = []
    for m in range(1, GROUP):
        q = plane(m)
        c = remote(part.at[q], part_recv.at[m], fin_ssem.at[m], fin_rsem.at[m], mate(m))
        c.start()
        fin_copies.append(c)
    final = part[p]
    for m in range(1, GROUP):
        fin_copies[m - 1].wait_recv()
        final = final + part_recv[m]
    lse_ref[...] = jnp.sum(final, 0, keepdims=True)

    for c in sends + sum_copies + cnt_copies + nl_copies:
        c.wait_send()
    for c in list(y_copies.values()) + list(z_copies.values()):
        c.wait_send()
    for c in ag_copies + own_copies + fwd_copies + fin_copies:
        c.wait_send()


def settle(direction, nlw, lse, direction_out, nlw_out, lse_out):
    direction_out[...] = direction[...]
    nlw_out[...] = nlw[...]
    lse_out[...] = jnp.log(lse[...])


def local(n, embeddings, centroids, log_weights):
    rows, depth = embeddings.shape
    total = centroids.shape[0]
    zs = n // GROUP
    comp = total // n
    comps = zs * comp
    dchunk = 256
    chunks = depth // dchunk
    grows = GROUP * rows
    reps = zs // 2
    hc = comp // 2
    dma = pltpu.SemaphoreType.DMA
    vmem = pl.BlockSpec(memory_space=pltpu.VMEM)
    bf16, f32 = jnp.bfloat16, jnp.float32
    direction, nlw, lse = pl.pallas_call(
        functools.partial(kernel, reps, n * rows, dchunk),
        out_shape=(
            jax.ShapeDtypeStruct((comp, depth), bf16),
            jax.ShapeDtypeStruct((1, comp), f32),
            jax.ShapeDtypeStruct((1, rows), f32),
        ),
        in_specs=[vmem, pl.BlockSpec(memory_space=pl.ANY), vmem],
        out_specs=(vmem, vmem, vmem),
        scratch_shapes=[
            pltpu.VMEM((grows, depth), bf16),
            pltpu.VMEM((comps, depth), bf16),
            pltpu.VMEM((comps, grows), f32),
            pltpu.VMEM((comps, grows), bf16),
            pltpu.VMEM((2 * GROUP, rows // 2), f32),
            pltpu.VMEM((GROUP, 2 * GROUP, rows // 2), f32),
            pltpu.VMEM((2, chunks, reps * hc, dchunk), bf16),
            pltpu.VMEM((2, chunks, reps * hc, dchunk), bf16),
            pltpu.VMEM((2, chunks, reps, hc, dchunk), bf16),
            pltpu.VMEM((2, chunks, reps, hc, dchunk), bf16),
            pltpu.VMEM((zs, 8, 128), f32),
            pltpu.VMEM((zs, 8, 128), f32),
            pltpu.VMEM((comp, depth), f32),
            pltpu.VMEM((zs, comp, depth), bf16),
            pltpu.VMEM((zs, 8, 128), f32),
            pltpu.VMEM((GROUP, 8, rows), f32),
            pltpu.VMEM((GROUP, 8, rows), f32),
            pltpu.VMEM((8, 128), f32),
            pltpu.VMEM((comps, 1), f32),
            dma((2, zs)),
            dma((GROUP, 2)), dma((GROUP, 2)),
            dma((2, chunks)), dma((2, chunks)),
            dma((2, chunks, reps)), dma((2, chunks, reps)),
            dma((GROUP,)), dma((GROUP,)),
            dma((zs,)), dma((zs,)),
            dma((reps, 2)), dma((reps, 2)),
            dma((2,)), dma((2,)),
            dma((reps, 2)), dma((reps, 2)),
            dma((zs,)), dma((zs,)),
            dma((GROUP,)), dma((GROUP,)),
        ],
        compiler_params=pltpu.CompilerParams(
            collective_id=0, has_side_effects=True, vmem_limit_bytes=60 * 1024 * 1024
        ),
    )(embeddings, centroids, log_weights.reshape(n, comp))
    direction, nlw, lse = pl.pallas_call(
        settle,
        out_shape=(
            jax.ShapeDtypeStruct((comp, depth), bf16),
            jax.ShapeDtypeStruct((1, comp), f32),
            jax.ShapeDtypeStruct((1, rows), f32),
        ),
        in_specs=[vmem, vmem, vmem],
        out_specs=(vmem, vmem, vmem),
    )(direction, nlw, lse)
    return direction, nlw.reshape(comp), lse.reshape(rows)


def solution(mesh):
    return jax.shard_map(
        functools.partial(local, mesh.shape["rows"]),
        mesh=mesh,
        in_specs=(P(("grp", "rows"), None), P(), P()),
        out_specs=(P(("grp", "rows"), None), P(("grp", "rows")), P(("grp", "rows"))),
        check_vma=False,
    )
```

```python
import functools

import jax
import jax.numpy as jnp
from jax import lax
from jax.experimental import pallas as pl
from jax.experimental.pallas import tpu as pltpu
from jax.sharding import PartitionSpec as P

KAPPA = 32
GROUP = 8
MESH = pl.DeviceIdType.MESH
NT = (((1,), (1,)), ((), ()))


def kernel(
    reps, nrows, dchunk, emb_ref, cent_hbm, lw_ref, dir_ref, nlw_ref, lse_ref,
    unit, cent, expo, resp, rsum, rsum_all, y_send, y_recv, z_send, z_recv, cnt_send, cnt_recv,
    own_sum, gathered, nlw_all, part, part_recv, lw_row, lw_col,
    cent_sem, row_ssem, row_rsem, y_ssem, y_rsem, z_ssem, z_rsem, sc_ssem, sc_rsem,
    cn_ssem, cn_rsem, ag_ssem, ag_rsem, own_ssem, own_rsem, fwd_ssem, fwd_rsem,
    nl_ssem, nl_rsem, fin_ssem, fin_rsem,
):
    rows, depth = emb_ref.shape
    half = rows // 2
    comp = dir_ref.shape[0]
    chunks = depth // dchunk
    zs = 2 * reps
    hc = comp // 2
    me = lax.axis_index("rows")
    p = me % 4 + 4 * ((me // 8) % 2)
    y = (me // 4) % 2
    h = me // 16
    mine = y * reps + h

    def plane(mask):
        q = p
        for bit in (1, 2, 4):
            if mask & bit:
                q = q + bit - 2 * bit * ((p // bit) % 2)
        return q

    def rank(q, yy, hh):
        return q % 4 + 4 * yy + 8 * (q // 4) + 16 * hh

    def dev(q, yy, hh):
        return {"rows": rank(q, yy, hh)}

    def mate(mask):
        return dev(plane(mask), y, h)

    def replica(o):
        b = (mine + o) % zs
        return dev(p, b // reps, b % reps)

    def remote(src, dst, ssem, rsem, to):
        return pltpu.make_async_remote_copy(
            src_ref=src, dst_ref=dst, send_sem=ssem, recv_sem=rsem,
            device_id=to, device_id_type=MESH,
        )

    barrier = pltpu.get_barrier_semaphore()
    for mask in range(1, GROUP):
        pl.semaphore_signal(barrier, inc=1, device_id=mate(mask), device_id_type=MESH)
    for o in range(1, zs):
        pl.semaphore_signal(barrier, inc=1, device_id=replica(o), device_id_type=MESH)

    cent_copies = [
        pltpu.make_async_copy(
            cent_hbm.at[pl.ds(rank(p, b // reps, b % reps) * comp + c * hc, hc)],
            cent.at[pl.ds((c * zs + b) * hc, hc)],
            cent_sem.at[c, b],
        )
        for c in range(2)
        for b in range(zs)
    ]
    for c in cent_copies:
        c.start()

    def column(row):
        return jnp.transpose(jnp.broadcast_to(row, (128, 128)))[:comp, :1]

    def unit_half(hf):
        here = pl.ds(hf * half, half)
        embed = emb_ref[here, :].astype(jnp.float32)
        unit[pl.ds(pl.multiple_of(p * rows + hf * half, half), half), :] = (
            embed * lax.rsqrt(jnp.sum(embed * embed, 1, keepdims=True) + 1e-06)
        ).astype(jnp.bfloat16)

    unit_half(0)
    pl.semaphore_wait(barrier, GROUP - 1 + zs - 1)

    def row_copy(dst, blk, hf):
        where = unit.at[pl.ds(plane(blk) * rows + hf * half, half)]
        m = blk ^ dst
        return remote(
            where, where, row_ssem.at[m, hf], row_rsem.at[m, hf], mate(dst)
        )

    def arrived(m, hf):
        where = unit.at[pl.ds(plane(m) * rows + hf * half, half)]
        remote(where, where, row_ssem.at[m, hf], row_rsem.at[m, hf], mate(1)).wait_recv()

    sends = []

    def send(dst, blk, hf):
        c = row_copy(dst, blk, hf)
        c.start()
        sends.append(c)

    for hf in (0, 1):
        if hf:
            unit_half(hf)
        send(2, 0, hf)
        send(4, 0, hf)
        send(1, 0, hf)
    for b in range(zs):
        lw_row[:1, :comp] = lw_ref[pl.ds(rank(p, b // reps, b % reps), 1), :]
        col = column(lw_row[:1, :])
        for c in range(2):
            lw_col[pl.ds((c * zs + b) * hc, hc), :] = col[c * hc : (c + 1) * hc]
    for c in cent_copies:
        c.wait()

    def score(m, hf):
        base = plane(m) * rows + hf * half
        at = pl.ds(pl.multiple_of(base, half), half)
        dots = lax.dot_general(cent[...], unit[at, :], NT, preferred_element_type=jnp.float32)
        e = jnp.exp(KAPPA * dots + lw_col[...])
        expo[:, at] = e
        rsum[pl.ds(plane(m) * 2 + hf, 1), :] = jnp.sum(e, 0, keepdims=True)

    score(0, 0)
    score(0, 1)
    arrived(2, 0)
    send(4, 2, 0)
    send(1, 2, 0)
    arrived(4, 1)
    send(2, 4, 1)
    send(1, 4, 1)
    for hf in (0, 1):
        arrived(1, hf)
        score(1, hf)
    score(2, 0)
    score(4, 1)
    arrived(2, 1)
    send(1, 2, 1)
    arrived(4, 0)
    send(1, 4, 0)
    score(2, 1)
    score(4, 0)
    for m, hf in ((3, 0), (5, 1), (3, 1), (5, 0)):
        arrived(m, hf)
        score(m, hf)
    for hf in (0, 1):
        arrived(6, hf)
        send(1, 6, hf)
    for hf in (0, 1):
        score(6, hf)
    for hf in (0, 1):
        arrived(7, hf)
        score(7, hf)

    sum_copies = []
    for m in range(1, GROUP):
        c = remote(rsum, rsum_all.at[m], sc_ssem.at[m], sc_rsem.at[m], mate(m))
        c.start()
        sum_copies.append(c)
    for c in sum_copies:
        c.wait_recv()
    total = rsum[...]
    for m in range(1, GROUP):
        total = total + rsum_all[m]
    rsum_all[0] = 1.0 / total

    def normalise(i, carry):
        at = pl.ds(pl.multiple_of(i * half, half), half)
        inv = rsum_all[0, pl.ds(i, 1), :]
        resp[:, at] = (expo[:, at] * inv).astype(jnp.bfloat16)
        return carry

    lax.fori_loop(0, 2 * GROUP, normalise, 0)

    side = reps * hc
    y_copies = {}
    def both(c, d, hh):
        cols = pl.ds(d * dchunk, dchunk)
        kept = expo[pl.ds(pl.multiple_of(c * zs * hc + y * side + hh * hc, hc), hc), cols]
        return kept + y_recv[c, d, pl.ds(pl.multiple_of(hh * hc, hc), hc), :].astype(jnp.float32)

    z_copies = {}

    def over_z(c, d):
        y_copies[c, d].wait_recv()
        for o in range(1, reps):
            hh = (h + o) % reps
            z_send[c, d, o] = both(c, d, hh).astype(jnp.bfloat16)
            z_copies[c, d, o] = remote(
                z_send.at[c, d, o], z_recv.at[c, d, o], z_ssem.at[c, d, o],
                z_rsem.at[c, d, o], dev(p, y, hh),
            )
            z_copies[c, d, o].start()
        own_sum[pl.ds(c * hc, hc), pl.ds(d * dchunk, dchunk)] = both(c, d, h)

    for c in range(2):
        for d in range(chunks):
            cols = pl.ds(d * dchunk, dchunk)
            expo[pl.ds(c * zs * hc, zs * hc), cols] = jnp.dot(
                resp[pl.ds(c * zs * hc, zs * hc), :], unit[:, cols],
                preferred_element_type=jnp.float32,
            )
            other = pl.ds(pl.multiple_of(c * zs * hc + (1 - y) * side, side), side)
            y_send[c, d] = expo[other, cols].astype(jnp.bfloat16)
            y_copies[c, d] = remote(
                y_send.at[c, d], y_recv.at[c, d], y_ssem.at[c, d], y_rsem.at[c, d],
                dev(p, 1 - y, h),
            )
            y_copies[c, d].start()
            if c:
                over_z(0, d)

    def piece(b, c):
        return gathered.at[b, pl.ds(c * hc, hc)]

    ag_copies = []
    own_copies = []

    def finish(c):
        here = pl.ds(c * hc, hc)
        square = jnp.zeros((hc, 1), jnp.float32)
        for d in range(chunks):
            cols = pl.ds(d * dchunk, dchunk)
            got = own_sum[here, cols]
            for o in range(1, reps):
                z_copies[c, d, o].wait_recv()
                got = got + z_recv[c, d, o].astype(jnp.float32)
            own_sum[here, cols] = got
            square = square + jnp.sum(got * got, 1, keepdims=True)
        direction = (own_sum[here, :] * lax.rsqrt(square + 1e-06)).astype(jnp.bfloat16)
        gathered[mine, here, :] = direction
        dir_ref[here, :] = direction
        where = piece(mine, c)
        for o in range(1, reps):
            copy = remote(
                where, where, ag_ssem.at[o, c], ag_rsem.at[o, c], dev(p, y, (h + o) % reps)
            )
            copy.start()
            ag_copies.append(copy)
        copy = remote(where, where, own_ssem.at[c], own_rsem.at[c], dev(p, 1 - y, h))
        copy.start()
        own_copies.append(copy)

    finish(0)
    cnt_copies = []
    ones = jnp.ones((8, GROUP * rows), jnp.bfloat16)
    for b in range(zs):
        for c in range(2):
            cnt_send[b, :, c * hc : (c + 1) * hc] = lax.dot_general(
                ones, resp[pl.ds((c * zs + b) * hc, hc), :], NT,
                preferred_element_type=jnp.float32,
            )
    for o in range(1, zs):
        to = (mine + o) % zs
        c = remote(cnt_send.at[to], cnt_recv.at[o], cn_ssem.at[o], cn_rsem.at[o], replica(o))
        c.start()
        cnt_copies.append(c)
    for d in range(chunks):
        over_z(1, d)
    finish(1)
    for c in cnt_copies:
        c.wait_recv()
    count = cnt_send[mine]
    for o in range(1, zs):
        count = count + cnt_recv[o]
    nlw = jnp.log(count[:, :comp] / nrows)
    nlw_all[mine, :, :comp] = nlw
    nlw_ref[...] = nlw[:1]
    nl_copies = []
    for o in range(1, zs):
        c = remote(
            nlw_all.at[mine], nlw_all.at[mine], nl_ssem.at[o], nl_rsem.at[o], replica(o)
        )
        c.start()
        nl_copies.append(c)

    part[...] = jnp.zeros_like(part)

    def second(b):
        col = column(nlw_all[b, :1, :])

        def body(i, carry):
            at = pl.ds(pl.multiple_of(i * rows, rows), rows)
            dots = lax.dot_general(
                gathered[b], unit[at, :], NT, preferred_element_type=jnp.float32
            )
            e = jnp.exp(KAPPA * dots + col)
            part[i] = part[i] + jnp.sum(e.reshape(comp // 8, 8, rows), 0)
            return carry

        lax.fori_loop(0, GROUP, body, 0)

    fwd_copies = []

    def forward(hf):
        for o in range(1, reps):
            where = piece(y * reps + (h + reps - o) % reps, hf)
            remote(where, where, ag_ssem.at[o, hf], ag_rsem.at[o, hf], dev(p, y, (h + o) % reps)).wait_recv()
            c = remote(
                where, where, fwd_ssem.at[o, hf], fwd_rsem.at[o, hf], dev(p, 1 - y, h)
            )
            c.start()
            fwd_copies.append(c)

    forward(0)
    second(mine)
    for c in nl_copies + own_copies:
        c.wait_recv()
    second((1 - y) * reps + h)
    forward(1)
    for o in range(1, reps):
        second(y * reps + (h + reps - o) % reps)
    for o in range(1, reps):
        b = (1 - y) * reps + (h + reps - o) % reps
        for hf in range(2):
            where = piece(b, hf)
            remote(where, where, fwd_ssem.at[o, hf], fwd_rsem.at[o, hf], dev(p, 1 - y, h)).wait_recv()
        second(b)

    fin_copies = []
    for m in range(1, GROUP):
        q = plane(m)
        c = remote(part.at[q], part_recv.at[m], fin_ssem.at[m], fin_rsem.at[m], mate(m))
        c.start()
        fin_copies.append(c)
    final = part[p]
    for m in range(1, GROUP):
        fin_copies[m - 1].wait_recv()
        final = final + part_recv[m]
    lse_ref[...] = jnp.sum(final, 0, keepdims=True)

    for c in sends + sum_copies + cnt_copies + nl_copies:
        c.wait_send()
    for c in list(y_copies.values()) + list(z_copies.values()):
        c.wait_send()
    for c in ag_copies + own_copies + fwd_copies + fin_copies:
        c.wait_send()


def settle(direction, nlw, lse, direction_out, nlw_out, lse_out):
    direction_out[...] = direction[...]
    nlw_out[...] = nlw[...]
    lse_out[...] = jnp.log(lse[...])


def local(n, embeddings, centroids, log_weights):
    rows, depth = embeddings.shape
    total = centroids.shape[0]
    zs = n // GROUP
    comp = total // n
    comps = zs * comp
    dchunk = 256
    chunks = depth // dchunk
    grows = GROUP * rows
    reps = zs // 2
    hc = comp // 2
    dma = pltpu.SemaphoreType.DMA
    vmem = pl.BlockSpec(memory_space=pltpu.VMEM)
    bf16, f32 = jnp.bfloat16, jnp.float32
    direction, nlw, lse = pl.pallas_call(
        functools.partial(kernel, reps, n * rows, dchunk),
        out_shape=(
            jax.ShapeDtypeStruct((comp, depth), bf16),
            jax.ShapeDtypeStruct((1, comp), f32),
            jax.ShapeDtypeStruct((1, rows), f32),
        ),
        in_specs=[vmem, pl.BlockSpec(memory_space=pl.ANY), vmem],
        out_specs=(vmem, vmem, vmem),
        scratch_shapes=[
            pltpu.VMEM((grows, depth), bf16),
            pltpu.VMEM((comps, depth), bf16),
            pltpu.VMEM((comps, grows), f32),
            pltpu.VMEM((comps, grows), bf16),
            pltpu.VMEM((2 * GROUP, rows // 2), f32),
            pltpu.VMEM((GROUP, 2 * GROUP, rows // 2), f32),
            pltpu.VMEM((2, chunks, reps * hc, dchunk), bf16),
            pltpu.VMEM((2, chunks, reps * hc, dchunk), bf16),
            pltpu.VMEM((2, chunks, reps, hc, dchunk), bf16),
            pltpu.VMEM((2, chunks, reps, hc, dchunk), bf16),
            pltpu.VMEM((zs, 8, 128), f32),
            pltpu.VMEM((zs, 8, 128), f32),
            pltpu.VMEM((comp, depth), f32),
            pltpu.VMEM((zs, comp, depth), bf16),
            pltpu.VMEM((zs, 8, 128), f32),
            pltpu.VMEM((GROUP, 8, rows), f32),
            pltpu.VMEM((GROUP, 8, rows), f32),
            pltpu.VMEM((8, 128), f32),
            pltpu.VMEM((comps, 1), f32),
            dma((2, zs)),
            dma((GROUP, 2)), dma((GROUP, 2)),
            dma((2, chunks)), dma((2, chunks)),
            dma((2, chunks, reps)), dma((2, chunks, reps)),
            dma((GROUP,)), dma((GROUP,)),
            dma((zs,)), dma((zs,)),
            dma((reps, 2)), dma((reps, 2)),
            dma((2,)), dma((2,)),
            dma((reps, 2)), dma((reps, 2)),
            dma((zs,)), dma((zs,)),
            dma((GROUP,)), dma((GROUP,)),
        ],
        compiler_params=pltpu.CompilerParams(
            collective_id=0, has_side_effects=True, vmem_limit_bytes=60 * 1024 * 1024
        ),
    )(embeddings, centroids, log_weights.reshape(n, comp))
    direction, nlw, lse = pl.pallas_call(
        settle,
        out_shape=(
            jax.ShapeDtypeStruct((comp, depth), bf16),
            jax.ShapeDtypeStruct((1, comp), f32),
            jax.ShapeDtypeStruct((1, rows), f32),
        ),
        in_specs=[vmem, vmem, vmem],
        out_specs=(vmem, vmem, vmem),
    )(direction, nlw, lse)
    return direction, nlw.reshape(comp), lse.reshape(rows)


def solution(mesh):
    return jax.shard_map(
        functools.partial(local, mesh.shape["rows"]),
        mesh=mesh,
        in_specs=(P(("grp", "rows"), None), P(), P()),
        out_specs=(P(("grp", "rows"), None), P(("grp", "rows")), P(("grp", "rows"))),
        check_vma=False,
    )
```
